1024 devices in a mesh: freq: 32 (over y, x_hi), tm: 32 (over x_lo, z, core).
Axes of the slice: x: 8 (x_hi: 4, x_lo: 2; x = x_hi * 2 + x_lo), y: 8, z: 8, core: 2. Of those that a mesh axis runs over, the one named last changes fastest.
Arguments:
- visibilities: bfloat16 [32, 32, 2, 512, 512], P('freq', 'tm'), may hold values from -1.796875 to 1.796875
- model_vis: bfloat16 [32, 8, 2, 512, 512], P('freq'), may hold values from -0.1796875 to 0.1796875
- station_flags: int32 [32, 32, 512], P('freq', 'tm'), may hold values 0 or 1
- initial_gains: float32 [32, 32, 2, 8, 512], P('freq', 'tm'), may hold values from -6 to 6
- initial_duals: float32 [32, 32, 2, 8, 512], P('freq', 'tm'), may hold values from -1.8 to 1.8
Outputs:
- solved_gains: float32 [32, 32, 2, 8, 512], P('freq', 'tm')
- consensus: float32 [32, 32, 2, 8, 512], P('freq', 'tm')
- final_duals: float32 [32, 32, 2, 8, 512], P('freq', 'tm')
The draws below stay inside these ranges and needn't reach their ends.
All inputs are finite; a program needn't handle non-finite values. No bound on the sum of `station_flags` on one device may be relied on, other than what follows from the above.
Results may differ from the reference program's by a relative error of at most 0.0003.
Values sent between devices are 32-bit elements; how exact they have to be, the bound alone decides.
A program may use at most 32 MiB of HBM per device.

```python
import math
import jax
import jax.numpy as jnp
from jax import lax

DIRS = 8
ITERS = 2
NR = 512
NF = 32
NT = 32
N_FREQ = 32
N_TM = 32


def touch_ends(array, rng, smallest, largest):
    place = [jax.random.randint(jax.random.fold_in(rng, axis), (), 0, length) for axis, length in enumerate(array.shape)]
    widest = array.shape.index(max(array.shape))
    next_to = place[:widest] + [(place[widest] + 1) % array.shape[widest]] + place[widest + 1:]
    return array.at[tuple(place)].set(smallest).at[tuple(next_to)].set(largest)


def level_of(key, extent, shards, least, high):
    def one(axis_at, blocks):
        draws = jax.random.uniform(jax.random.fold_in(jax.random.fold_in(key, 6), axis_at), (blocks,), jnp.float32, least / len(shards), high / len(shards))
        return jnp.repeat(jnp.exp(draws), extent[axis_at] // blocks).reshape((-1,) + (1,) * (len(extent) - axis_at - 1))

    loudness = one(*shards[0])
    for cut in shards[1:]:
        loudness = loudness * one(*cut)
    return loudness


def normal_values(stream_key, dims, scale, limit, pieces=(), held_as=jnp.bfloat16):
    result = jax.random.normal(stream_key, dims, jnp.float32) * scale
    if len(pieces) > 0:
        result = level_of(stream_key, dims, pieces, -0.22, 0.18) * result
    return jnp.clip(result, min=-limit, max=limit).astype(held_as)


def setup_inputs(seed: int = 0) -> dict:
    splits = jax.random.split(jax.random.key(seed), 6)
    visibilities = normal_values(splits[0], (NF, NT, 2, NR, NR), 0.3, 1.796875, ((0, 32), (1, 32)))
    model_vis = normal_values(splits[1], (NF, DIRS, 2, NR, NR), 0.03, 0.1796875, ((0, 32),))
    station_flags = touch_ends((jax.random.randint(splits[2], (NF, NT, NR), 0, 16) < 15).astype(jnp.int32), jax.random.fold_in(splits[2], 1), 0, 1)
    initial_gains = normal_values(splits[3], (NF, NT, 2, DIRS, NR), 1.0, 6.0, ((0, 32), (1, 32)), jnp.float32)
    initial_duals = normal_values(splits[4], (NF, NT, 2, DIRS, NR), 0.3, 1.8, ((0, 32), (1, 32)), jnp.float32)
    return {"visibilities": visibilities, "model_vis": model_vis, "station_flags": station_flags, "initial_gains": initial_gains, "initial_duals": initial_duals}


penalty = 1.0

def poly_basis(length, position, order_count):
    centre = position - (length - 1) / 2.0
    constant = jnp.ones_like(position) / math.sqrt(length)
    linear = centre / math.sqrt(length * (length * length - 1) / 12.0)
    stacked = [constant, linear]
    if order_count == 3:
        quadratic = (centre * centre - (length * length - 1) / 12.0) / math.sqrt(length * (length * length - 1) * (length * length - 4) / 180.0)
        stacked.append(quadratic)
    return jnp.stack(stacked, axis=0)

def local_solve(vis_block, model_block, flag_block, gains_block, target_block):
    real_vis = vis_block[0].astype(jnp.float32)
    imag_vis = vis_block[1].astype(jnp.float32)
    model_real = model_block[:, 0].astype(jnp.float32)
    model_imag = model_block[:, 1].astype(jnp.float32)
    gain_real = gains_block[0]
    gain_imag = gains_block[1]
    weight = flag_block.astype(jnp.float32)
    outer_real = gain_real[:, :, None] * gain_real[:, None, :] + gain_imag[:, :, None] * gain_imag[:, None, :]
    outer_imag = gain_imag[:, :, None] * gain_real[:, None, :] - gain_real[:, :, None] * gain_imag[:, None, :]
    pred_real = lax.optimization_barrier(jnp.sum(model_real * outer_real - model_imag * outer_imag, axis=0))
    pred_imag = lax.optimization_barrier(jnp.sum(model_real * outer_imag + model_imag * outer_real, axis=0))
    pair_weight = weight[:, None] * weight[None, :]
    resid_real = (real_vis - pred_real) * pair_weight
    resid_imag = (imag_vis - pred_imag) * pair_weight
    proj_real = model_real * gain_real[:, None, :] + model_imag * gain_imag[:, None, :]
    proj_imag = model_real * gain_imag[:, None, :] - model_imag * gain_real[:, None, :]
    numer_real = lax.optimization_barrier(jnp.sum(resid_real[None] * proj_real - resid_imag[None] * proj_imag, axis=2))
    numer_imag = lax.optimization_barrier(jnp.sum(resid_real[None] * proj_imag + resid_imag[None] * proj_real, axis=2))
    gain_power = (gain_real * gain_real + gain_imag * gain_imag) * weight
    curvature = weight[None, :] * lax.optimization_barrier(jnp.sum((model_real * model_real + model_imag * model_imag) * gain_power[:, None, :], axis=2))
    divisor = curvature + penalty
    new_real = (numer_real + curvature * gain_real + penalty * target_block[0]) / divisor
    new_imag = (numer_imag + curvature * gain_imag + penalty * target_block[1]) / divisor
    return jnp.stack([new_real, new_imag], axis=0)

def solve_all(visibilities, model_vis, station_flags, current, target):

    def one_block(block_index):
        freq_place = block_index // N_TM
        time_place = block_index % N_TM
        return local_solve(visibilities[freq_place, time_place], model_vis[freq_place], station_flags[freq_place, time_place], current[freq_place, time_place], target[freq_place, time_place])
    solved = lax.map(one_block, jnp.arange(N_FREQ * N_TM, dtype=jnp.int32))
    return solved.reshape(current.shape)

def reference(visibilities, model_vis, station_flags, initial_gains, initial_duals):
    freq_basis = poly_basis(N_FREQ, jnp.arange(N_FREQ).astype(jnp.float32), 3)
    time_basis = poly_basis(N_TM, jnp.arange(N_TM).astype(jnp.float32), 2)
    current = initial_gains
    scaled_dual = initial_duals
    consensus = initial_gains
    for iteration in range(ITERS):
        merged = (current + scaled_dual).reshape(N_FREQ, N_TM, -1)
        coeffs = jnp.einsum('if,jt,ftx->ijx', freq_basis, time_basis, merged, precision=lax.Precision.HIGHEST)
        consensus = jnp.einsum('if,jt,ijx->ftx', freq_basis, time_basis, coeffs, precision=lax.Precision.HIGHEST).reshape(current.shape)
        scaled_dual = scaled_dual + current - consensus
        target = consensus - scaled_dual
        current = solve_all(visibilities, model_vis, station_flags, current, target)
    return (current, consensus, scaled_dual)
```

```python
import math

import jax
import jax.numpy as jnp
from jax import lax
from jax.experimental import pallas as pl
from jax.experimental.pallas import tpu as pltpu
from jax.sharding import PartitionSpec as P

DIRS = 8
NR = 512
LANES = 128
TILES = NR // LANES
ROWS = 16
BLOCKS = NR // ROWS
LOADS = 4
N_Y, N_XH, N_XL, N_ZC = 8, 4, 2, 16
N_X = N_XH * N_XL
N_Z = N_ZC // 2
NF = N_Y * N_XH
NT = N_XL * N_ZC
MESH = pl.DeviceIdType.MESH
FAR_FIRST = (4, 3, 5, 2, 6, 1, 7)

F0 = 1.0 / math.sqrt(NF)
F1 = 1.0 / math.sqrt(NF * (NF * NF - 1) / 12.0)
F2 = 1.0 / math.sqrt(NF * (NF * NF - 1) * (NF * NF - 4) / 180.0)
F2_SHIFT = (NF * NF - 1) / 12.0
T0 = 1.0 / math.sqrt(NT)
T1 = 1.0 / math.sqrt(NT * (NT * NT - 1) / 12.0)


def tile(index):
    return pl.ds(index * LANES, LANES)


def to_owner_rows(source, target, first_row):
    for lane_tile in range(TILES):
        for pair in range(DIRS // 2):
            for part in range(2):
                target[lane_tile * 4 + pair, first_row + 2 * part : first_row + 2 * part + 2, :] = source[
                    part, 2 * pair : 2 * pair + 2, tile(lane_tile)
                ]


def from_owner_rows(source, target):
    for lane_tile in range(TILES):
        for pair in range(DIRS // 2):
            for part in range(2):
                target[part, 2 * pair : 2 * pair + 2, tile(lane_tile)] = source[
                    lane_tile * 4 + pair, 2 * part : 2 * part + 2, :
                ]


def add_all(terms):
    while len(terms) > 1:
        terms = [a + b for a, b in zip(terms[::2], terms[1::2])] + terms[len(terms) // 2 * 2 :]
    return terms[0]


def kernel(
    vis_hbm, model_hbm, flag_ref, gains_ref, duals_ref,
    out_gains, out_consensus, out_duals,
    model_v, vis_v, masked_v, column_v, stack_v, d_v, sums_v, numer_v, merged_v, work_v, spare_v, eval_v,
    send_z, recv_z, send_w, recv_w, send_x, recv_x, send_y, recv_y, send_g, recv_g,
    load_sem, z_sem, w_sem, x_sem, y_sem, g_sem,
):
    freq = lax.axis_index("freq")
    time = lax.axis_index("tm")
    y = freq // N_XH
    x_hi = lax.rem(freq, N_XH)
    x_lo = time // N_ZC
    zc = lax.rem(time, N_ZC)
    x = x_hi * N_XL + x_lo
    z = zc // 2
    core = lax.rem(zc, 2)

    def z_peer(step, flip):
        return lax.rem(z + step, N_Z) * 2 + lax.rem(core + flip, 2)

    z_peers = [z_peer(step, flip) for step in FAR_FIRST for flip in (0, 1)] + [z_peer(0, 1)]
    x_peers = [lax.rem(x + step, N_X) for step in FAR_FIRST]
    y_peers = [lax.rem(y + step, N_Y) for step in FAR_FIRST]

    def z_device(peer):
        return (freq, x_lo * N_ZC + peer)

    def x_device(peer):
        return (y * N_XH + peer // N_XL, lax.rem(peer, N_XL) * N_ZC + zc)

    def y_device(peer):
        return (peer * N_XH + x_hi, time)

    loads = []
    for part in range(LOADS):
        rows = pl.ds(part * (NR // LOADS), NR // LOADS)
        model_copy = pltpu.make_async_copy(
            model_hbm.at[0, :, :, rows, :], model_v.at[:, :, rows, :], load_sem.at[0, part]
        )
        vis_copy = pltpu.make_async_copy(vis_hbm.at[0, 0, :, rows, :], vis_v.at[:, rows, :], load_sem.at[1, part])
        model_copy.start()
        vis_copy.start()
        loads.append((model_copy, vis_copy))

    barrier = pltpu.get_barrier_semaphore()
    devices = [z_device(p) for p in z_peers] + [x_device(p) for p in x_peers] + [y_device(p) for p in y_peers]
    for device in devices:
        pl.semaphore_signal(barrier, inc=1, device_id=device, device_id_type=MESH)

    gains = gains_ref[0, 0]
    merged = gains + duals_ref[0, 0]
    merged_v[...] = merged
    to_owner_rows(merged_v, send_z, 0)
    mask = flag_ref[0].astype(jnp.float32)

    pl.semaphore_wait(barrier, len(devices))

    def scatter(source, target, sem, peers, device_of, slot):
        for peer in peers:
            pltpu.make_async_remote_copy(
                src_ref=source(peer),
                dst_ref=target.at[slot],
                send_sem=sem.at[0],
                recv_sem=sem.at[1],
                device_id=device_of(peer),
                device_id_type=MESH,
            ).start()

    def wait_bytes(buffer, count, sem):
        part = buffer.at[pl.ds(0, count)]
        pltpu.make_async_copy(part, part, sem).wait()

    def time_moments(parts):
        total = add_all(list(parts))
        ramp = add_all([(slot - (N_ZC - 1) / 2.0) * part for slot, part in enumerate(parts)])
        shift = (x_lo * N_ZC).astype(jnp.float32) - (NT - N_ZC) / 2.0
        return total * T0, (ramp + shift * total) * T1

    def freq_weights(place):
        centre = place.astype(jnp.float32) - (NF - 1) / 2.0
        return F0, centre * F1, (centre * centre - F2_SHIFT) * F2

    def start_x(turn, parts):
        first, second = time_moments(parts)
        send_x[turn, 0:4, :] = first
        send_x[turn, 4:8, :] = second
        scatter(lambda peer: send_x.at[turn], recv_x.at[turn], x_sem.at[turn], x_peers, x_device, x)
        recv_x[turn, x] = send_x[turn]

    def start_y(turn):
        wait_bytes(recv_x.at[turn], N_X - 1, x_sem.at[turn, 1])
        pairs = [recv_x[turn, N_XL * h] + recv_x[turn, N_XL * h + 1] for h in range(N_XH)]
        weights = [freq_weights(y * N_XH + h) for h in range(N_XH)]
        for order in range(3):
            send_y[turn, order] = add_all([weights[h][order] * pairs[h] for h in range(N_XH)])
        scatter(lambda peer: send_y.at[turn], recv_y.at[turn], y_sem.at[turn], y_peers, y_device, y)
        recv_y[turn, y] = send_y[turn]

    def evaluate(turn):
        wait_bytes(recv_y.at[turn], N_Y - 1, y_sem.at[turn, 1])
        weights = freq_weights(freq)
        coeffs = [add_all([recv_y[turn, h, order] for h in range(N_Y)]) for order in range(3)]
        eval_v[...] = add_all([weights[order] * coeffs[order] for order in range(3)])
        constant = eval_v[0:4, :] * T0
        slope = eval_v[4:8, :] * T1
        shift = (x_lo * N_ZC).astype(jnp.float32) - (NT - 1) / 2.0
        base = constant + shift * slope
        return [base + float(slot) * slope for slot in range(N_ZC)]

    def start_g(turn, values):
        for slot in range(N_ZC):
            send_g[turn, slot] = values[slot]
        scatter(lambda peer: send_g.at[turn, peer], recv_g.at[turn], g_sem.at[turn], z_peers, z_device, zc)
        recv_g[turn, zc] = send_g[turn, zc]

    def consensus_of(turn):
        wait_bytes(recv_g.at[turn], N_ZC - 1, g_sem.at[turn, 1])
        from_owner_rows(recv_g.at[turn], work_v)
        return work_v[...]

    lane = lax.broadcasted_iota(jnp.int32, (ROWS, LANES), 1)
    stack_v[...] = jnp.zeros_like(stack_v)

    def start_solve(current):
        masked_v[...] = current * mask[:, None, :]
        stack_v[0:DIRS, :] = current[0]
        stack_v[DIRS : 2 * DIRS, :] = current[1]
        column_v[...] = jnp.transpose(stack_v[...])

    def solve_rows(first, last):
        def block(index, carry):
            rows = pl.ds(pl.multiple_of(index * ROWS, ROWS), ROWS)
            column = column_v[rows, :]
            resid = []
            for q in range(TILES):
                pred_real = pred_imag = None
                for k in range(DIRS):
                    model_real = model_v[k, 0, rows, tile(q)].astype(jnp.float32)
                    model_imag = model_v[k, 1, rows, tile(q)].astype(jnp.float32)
                    row_real = masked_v[0, k : k + 1, tile(q)]
                    row_imag = masked_v[1, k : k + 1, tile(q)]
                    d_real = model_real * row_real + model_imag * row_imag
                    d_imag = model_imag * row_real - model_real * row_imag
                    d_v[k, 0, :, tile(q)] = d_real
                    d_v[k, 1, :, tile(q)] = d_imag
                    col_real = column[:, k : k + 1]
                    col_imag = column[:, DIRS + k : DIRS + k + 1]
                    term_real = col_real * d_real - col_imag * d_imag
                    term_imag = col_real * d_imag + col_imag * d_real
                    pred_real = term_real if pred_real is None else pred_real + term_real
                    pred_imag = term_imag if pred_imag is None else pred_imag + term_imag
                mask_row = mask[:, q * LANES : (q + 1) * LANES]
                resid.append(
                    (
                        vis_v[0, rows, tile(q)].astype(jnp.float32) * mask_row - pred_real,
                        vis_v[1, rows, tile(q)].astype(jnp.float32) * mask_row - pred_imag,
                    )
                )
            sums = jnp.zeros((ROWS, LANES), jnp.float32)
            for k in range(DIRS):
                numer_real, numer_imag, power = [], [], []
                for q in range(TILES):
                    d_real = d_v[k, 0, :, tile(q)]
                    d_imag = d_v[k, 1, :, tile(q)]
                    resid_real, resid_imag = resid[q]
                    numer_real.append(resid_real * d_real + resid_imag * d_imag)
                    numer_imag.append(resid_imag * d_real - resid_real * d_imag)
                    power.append(d_real * d_real + d_imag * d_imag)
                for place, terms in enumerate((numer_real, numer_imag, power)):
                    total = jnp.sum(add_all(terms), axis=1, keepdims=True)
                    sums = jnp.where(lane == place * DIRS + k, total, sums)
            sums_v[rows, :] = sums
            return carry

        lax.fori_loop(first, last, block, 0)

    def finish_solve(current):
        numer_v[...] = jnp.transpose(sums_v[...])
        curvature = numer_v[2 * DIRS : 3 * DIRS, :] * mask
        weight = 1.0 / (curvature + 1.0)
        return [numer_v[c * DIRS : (c + 1) * DIRS, :] * mask + curvature * current[c] for c in range(2)], weight

    scatter(lambda peer: send_z.at[peer], recv_z, z_sem, z_peers, z_device, zc)
    recv_z[zc] = send_z[zc]
    start_solve(gains)
    per_load = BLOCKS // LOADS
    for part in range(LOADS // 2):
        loads[part][0].wait()
        loads[part][1].wait()
        solve_rows(part * per_load, (part + 1) * per_load)
    wait_bytes(recv_z, N_ZC - 1, z_sem.at[1])
    start_x(0, [recv_z[slot] for slot in range(N_ZC)])
    for part in range(LOADS // 2, LOADS):
        loads[part][0].wait()
        loads[part][1].wait()
        solve_rows(part * per_load, (part + 1) * per_load)
    partial, weight = finish_solve(gains)
    for c in range(2):
        work_v[c] = weight * (partial[c] - merged_v[c]) + merged_v[c]
        spare_v[c] = 2.0 * weight - 1.0
    to_owner_rows(work_v, send_w, 0)
    to_owner_rows(spare_v, send_w, 4)
    scatter(lambda peer: send_w.at[peer], recv_w, w_sem, z_peers, z_device, zc)
    recv_w[zc] = send_w[zc]
    start_y(0)

    values = evaluate(0)
    wait_bytes(recv_w, N_ZC - 1, w_sem.at[1])
    start_x(1, [recv_w[slot, 0:4, :] + recv_w[slot, 4:8, :] * values[slot] for slot in range(N_ZC)])
    start_g(0, values)
    first = consensus_of(0)
    for c in range(2):
        gain = (partial[c] + 2.0 * first[c] - merged_v[c]) * weight
        spare_v[c] = gain
        merged_v[c] = gain + merged_v[c] - first[c]
    start_y(1)
    gains = spare_v[...]
    start_solve(gains)
    solve_rows(0, 3 * BLOCKS // 4)
    start_g(1, evaluate(1))
    solve_rows(3 * BLOCKS // 4, BLOCKS)
    partial, weight = finish_solve(spare_v)
    second = consensus_of(1)
    for c in range(2):
        merged = merged_v[c]
        out_consensus[0, 0, c] = second[c]
        out_duals[0, 0, c] = merged - second[c]
        out_gains[0, 0, c] = (partial[c] + 2.0 * second[c] - merged) * weight

    wait_bytes(recv_z, N_ZC - 1, z_sem.at[0])
    wait_bytes(recv_w, N_ZC - 1, w_sem.at[0])
    for turn in range(2):
        wait_bytes(recv_x.at[turn], N_X - 1, x_sem.at[turn, 0])
        wait_bytes(recv_y.at[turn], N_Y - 1, y_sem.at[turn, 0])
        wait_bytes(recv_g.at[turn], N_ZC - 1, g_sem.at[turn, 0])


def per_device(visibilities, model_vis, station_flags, initial_gains, initial_duals):
    block = jax.ShapeDtypeStruct((1, 1, 2, DIRS, NR), jnp.float32)
    f32 = jnp.float32
    vmem = pl.BlockSpec(memory_space=pltpu.VMEM)
    hbm = pl.BlockSpec(memory_space=pl.ANY)
    return pl.pallas_call(
        kernel,
        out_shape=(block, block, block),
        in_specs=[hbm, hbm, vmem, vmem, vmem],
        out_specs=(vmem, vmem, vmem),
        scratch_shapes=[
            pltpu.VMEM((DIRS, 2, NR, NR), jnp.bfloat16),
            pltpu.VMEM((2, NR, NR), jnp.bfloat16),
            pltpu.VMEM((2, DIRS, NR), f32),
            pltpu.VMEM((NR, LANES), f32),
            pltpu.VMEM((LANES, NR), f32),
            pltpu.VMEM((DIRS, 2, ROWS, NR), f32),
            pltpu.VMEM((NR, LANES), f32),
            pltpu.VMEM((LANES, NR), f32),
            pltpu.VMEM((2, DIRS, NR), f32),
            pltpu.VMEM((2, DIRS, NR), f32),
            pltpu.VMEM((2, DIRS, NR), f32),
            pltpu.VMEM((8, LANES), f32),
            pltpu.VMEM((N_ZC, 4, LANES), f32),
            pltpu.VMEM((N_ZC, 4, LANES), f32),
            pltpu.VMEM((N_ZC, 8, LANES), f32),
            pltpu.VMEM((N_ZC, 8, LANES), f32),
            pltpu.VMEM((2, 8, LANES), f32),
            pltpu.VMEM((2, N_X, 8, LANES), f32),
            pltpu.VMEM((2, 3, 8, LANES), f32),
            pltpu.VMEM((2, N_Y, 3, 8, LANES), f32),
            pltpu.VMEM((2, N_ZC, 4, LANES), f32),
            pltpu.VMEM((2, N_ZC, 4, LANES), f32),
            pltpu.SemaphoreType.DMA((2, LOADS)),
            pltpu.SemaphoreType.DMA((2,)),
            pltpu.SemaphoreType.DMA((2,)),
            pltpu.SemaphoreType.DMA((2, 2)),
            pltpu.SemaphoreType.DMA((2, 2)),
            pltpu.SemaphoreType.DMA((2, 2)),
        ],
        compiler_params=pltpu.CompilerParams(
            collective_id=0, has_side_effects=True, vmem_limit_bytes=60 * 1024 * 1024
        ),
    )(visibilities, model_vis, station_flags, initial_gains, initial_duals)


def solution(mesh):
    in_specs = (
        P("freq", "tm", None, None, None),
        P("freq", None, None, None, None),
        P("freq", "tm", None),
        P("freq", "tm", None, None, None),
        P("freq", "tm", None, None, None),
    )
    out_specs = (P("freq", "tm", None, None, None),) * 3
    return jax.shard_map(per_device, mesh=mesh, in_specs=in_specs, out_specs=out_specs, check_vma=False)
```

```python
import math

import jax
import jax.numpy as jnp
from jax import lax
from jax.experimental import pallas as pl
from jax.experimental.pallas import tpu as pltpu
from jax.sharding import PartitionSpec as P

DIRS = 8
NR = 512
LANES = 128
TILES = NR // LANES
ROWS = 16
BLOCKS = NR // ROWS
LOADS = 4
N_Y, N_XH, N_XL, N_ZC = 8, 4, 2, 16
N_X = N_XH * N_XL
N_Z = N_ZC // 2
NF = N_Y * N_XH
NT = N_XL * N_ZC
MESH = pl.DeviceIdType.MESH
FIRST_SPAN = 20
SECOND_SPAN = 18
FAR_FIRST = (4, 3, 5, 2, 6, 1, 7)

F0 = 1.0 / math.sqrt(NF)
F1 = 1.0 / math.sqrt(NF * (NF * NF - 1) / 12.0)
F2 = 1.0 / math.sqrt(NF * (NF * NF - 1) * (NF * NF - 4) / 180.0)
F2_SHIFT = (NF * NF - 1) / 12.0
T0 = 1.0 / math.sqrt(NT)
T1 = 1.0 / math.sqrt(NT * (NT * NT - 1) / 12.0)


def tile(index):
    return pl.ds(index * LANES, LANES)


def to_owner_rows(source, target, first_row):
    for lane_tile in range(TILES):
        for pair in range(DIRS // 2):
            for part in range(2):
                target[lane_tile * 4 + pair, first_row + 2 * part : first_row + 2 * part + 2, :] = source[
                    part, 2 * pair : 2 * pair + 2, tile(lane_tile)
                ]


def from_owner_rows(source, target):
    for lane_tile in range(TILES):
        for pair in range(DIRS // 2):
            for part in range(2):
                target[part, 2 * pair : 2 * pair + 2, tile(lane_tile)] = source[
                    lane_tile * 4 + pair, 2 * part : 2 * part + 2, :
                ]


def add_all(terms):
    while len(terms) > 1:
        terms = [a + b for a, b in zip(terms[::2], terms[1::2])] + terms[len(terms) // 2 * 2 :]
    return terms[0]


def kernel(
    vis_hbm, model_hbm, flag_hbm, gains_hbm, duals_hbm,
    out_v,
    model_v, vis_v, wide_v, square_v, flag_v, gains_v, duals_v,
    masked_v, power_v, column_v, stack_v, d_all, sums_v, numer_v, merged_v, work_v, spare_v, eval_v,
    send_z, recv_z, send_w, recv_w, send_x, recv_x, send_y, recv_y, send_g, recv_g,
    load_sem, small_sem, z_sem, w_sem, x_sem, y_sem, g_sem,
):
    freq = lax.axis_index("freq")
    time = lax.axis_index("tm")
    y = freq // N_XH
    x_hi = lax.rem(freq, N_XH)
    x_lo = time // N_ZC
    zc = lax.rem(time, N_ZC)
    x = x_hi * N_XL + x_lo
    z = zc // 2
    core = lax.rem(zc, 2)

    def z_peer(step, flip):
        return lax.rem(z + step, N_Z) * 2 + lax.rem(core + flip, 2)

    z_peers = [z_peer(step, flip) for step in FAR_FIRST for flip in (0, 1)] + [z_peer(0, 1)]
    x_peers = [lax.rem(x + step, N_X) for step in FAR_FIRST]
    y_peers = [lax.rem(y + step, N_Y) for step in FAR_FIRST]

    def z_device(peer):
        return (freq, x_lo * N_ZC + peer)

    def x_device(peer):
        return (y * N_XH + peer // N_XL, lax.rem(peer, N_XL) * N_ZC + zc)

    def y_device(peer):
        return (peer * N_XH + x_hi, time)

    barrier = pltpu.get_barrier_semaphore()
    devices = [z_device(p) for p in z_peers] + [x_device(p) for p in x_peers] + [y_device(p) for p in y_peers]
    small = [
        pltpu.make_async_copy(gains_hbm.at[0, 0], gains_v, small_sem.at[0]),
        pltpu.make_async_copy(duals_hbm.at[0, 0], duals_v, small_sem.at[1]),
        pltpu.make_async_copy(flag_hbm.at[0], flag_v, small_sem.at[2]),
    ]
    for copy in small:
        copy.start()
    for device in devices:
        pl.semaphore_signal(barrier, inc=1, device_id=device, device_id_type=MESH)

    loads = []
    for part in range(LOADS):
        rows = pl.ds(part * (NR // LOADS), NR // LOADS)
        model_copy = pltpu.make_async_copy(
            model_hbm.at[0, :, :, rows, :], model_v.at[:, :, rows, :], load_sem.at[0, part]
        )
        vis_copy = pltpu.make_async_copy(vis_hbm.at[0, 0, :, rows, :], vis_v.at[:, rows, :], load_sem.at[1, part])
        model_copy.start()
        vis_copy.start()
        loads.append((model_copy, vis_copy))

    for copy in small:
        copy.wait()
    merged_v[...] = gains_v[...] + duals_v[...]
    to_owner_rows(merged_v, send_z, 0)
    mask = flag_v[...].astype(jnp.float32)

    pl.semaphore_wait(barrier, len(devices))

    def scatter(source, target, sem, peers, device_of, slot):
        for peer in peers:
            pltpu.make_async_remote_copy(
                src_ref=source(peer),
                dst_ref=target.at[slot],
                send_sem=sem.at[0],
                recv_sem=sem.at[1],
                device_id=device_of(peer),
                device_id_type=MESH,
            ).start()

    def wait_bytes(buffer, count, sem):
        part = buffer.at[pl.ds(0, count)]
        pltpu.make_async_copy(part, part, sem).wait()

    def time_moments(parts):
        total = add_all(list(parts))
        ramp = add_all([(slot - (N_ZC - 1) / 2.0) * part for slot, part in enumerate(parts)])
        shift = (x_lo * N_ZC).astype(jnp.float32) - (NT - N_ZC) / 2.0
        return total * T0, (ramp + shift * total) * T1

    def freq_weights(place):
        centre = place.astype(jnp.float32) - (NF - 1) / 2.0
        return F0, centre * F1, (centre * centre - F2_SHIFT) * F2

    def start_x(turn, parts):
        first, second = time_moments(parts)
        send_x[turn, 0:4, :] = first
        send_x[turn, 4:8, :] = second
        scatter(lambda peer: send_x.at[turn], recv_x.at[turn], x_sem.at[turn], x_peers, x_device, x)
        recv_x[turn, x] = send_x[turn]

    def start_y(turn):
        wait_bytes(recv_x.at[turn], N_X - 1, x_sem.at[turn, 1])
        pairs = [recv_x[turn, N_XL * h] + recv_x[turn, N_XL * h + 1] for h in range(N_XH)]
        weights = [freq_weights(y * N_XH + h) for h in range(N_XH)]
        coeffs = [add_all([weights[h][order] * pairs[h] for h in range(N_XH)]) for order in range(3)]
        for peer in range(N_Y):
            there = freq_weights(peer * N_XH + x_hi)
            send_y[turn, peer] = add_all([there[order] * coeffs[order] for order in range(3)])
        scatter(lambda peer: send_y.at[turn, peer], recv_y.at[turn], y_sem.at[turn], y_peers, y_device, y)
        recv_y[turn, y] = send_y[turn, y]

    def evaluate(turn):
        wait_bytes(recv_y.at[turn], N_Y - 1, y_sem.at[turn, 1])
        eval_v[...] = add_all([recv_y[turn, h] for h in range(N_Y)])
        constant = eval_v[0:4, :] * T0
        slope = eval_v[4:8, :] * T1
        shift = (x_lo * N_ZC).astype(jnp.float32) - (NT - 1) / 2.0
        base = constant + shift * slope
        return [base + float(slot) * slope for slot in range(N_ZC)]

    def start_g(turn, values):
        for slot in range(N_ZC):
            send_g[turn, slot] = values[slot]
        scatter(lambda peer: send_g.at[turn, peer], recv_g.at[turn], g_sem.at[turn], z_peers, z_device, zc)
        recv_g[turn, zc] = send_g[turn, zc]

    def consensus_of(turn):
        wait_bytes(recv_g.at[turn], N_ZC - 1, g_sem.at[turn, 1])
        from_owner_rows(recv_g.at[turn], work_v)
        return work_v[...]

    stack_v[...] = jnp.zeros_like(stack_v)
    sums_v[...] = jnp.zeros_like(sums_v)

    def start_solve(current):
        masked_v[...] = current * mask[:, None, :]
        power_v[...] = (current[0] * current[0] + current[1] * current[1]) * mask
        stack_v[0:DIRS, :] = current[0]
        stack_v[DIRS : 2 * DIRS, :] = current[1]
        column_v[...] = jnp.transpose(stack_v[...])

    def solve_rows(first, last, keep):
        def block(index, d_v):
            rows = pl.ds(pl.multiple_of(index * ROWS, ROWS), ROWS)
            column = column_v[rows, :]
            resid = []
            for q in range(TILES):
                pred_real = pred_imag = None
                for k in range(DIRS):
                    if keep:
                        model_real = model_v[k, 0, rows, tile(q)].astype(jnp.float32)
                        model_imag = model_v[k, 1, rows, tile(q)].astype(jnp.float32)
                        wide_v[k, 0, rows, tile(q)] = model_real
                        wide_v[k, 1, rows, tile(q)] = model_imag
                        square_v[k, rows, tile(q)] = model_real * model_real + model_imag * model_imag
                    else:
                        model_real = wide_v[k, 0, rows, tile(q)]
                        model_imag = wide_v[k, 1, rows, tile(q)]
                    row_real = masked_v[0, k : k + 1, tile(q)]
                    row_imag = masked_v[1, k : k + 1, tile(q)]
                    d_real = model_real * row_real + model_imag * row_imag
                    d_imag = model_imag * row_real - model_real * row_imag
                    d_v[k, 0, :, tile(q)] = d_real
                    d_v[k, 1, :, tile(q)] = d_imag
                    col_real = column[:, k : k + 1]
                    col_imag = column[:, DIRS + k : DIRS + k + 1]
                    term_real = col_real * d_real - col_imag * d_imag
                    term_imag = col_real * d_imag + col_imag * d_real
                    pred_real = term_real if pred_real is None else pred_real + term_real
                    pred_imag = term_imag if pred_imag is None else pred_imag + term_imag
                mask_row = mask[:, q * LANES : (q + 1) * LANES]
                resid.append(
                    (
                        vis_v[0, rows, tile(q)].astype(jnp.float32) * mask_row - pred_real,
                        vis_v[1, rows, tile(q)].astype(jnp.float32) * mask_row - pred_imag,
                    )
                )
            for k in range(DIRS):
                numer_real, numer_imag, power = [], [], []
                for q in range(TILES):
                    d_real = d_v[k, 0, :, tile(q)]
                    d_imag = d_v[k, 1, :, tile(q)]
                    resid_real, resid_imag = resid[q]
                    numer_real.append(resid_real * d_real + resid_imag * d_imag)
                    numer_imag.append(resid_imag * d_real - resid_real * d_imag)
                    power.append(square_v[k, rows, tile(q)] * power_v[k : k + 1, tile(q)])
                for place, terms in enumerate((numer_real, numer_imag, power)):
                    lane = place * DIRS + k
                    sums_v[rows, lane : lane + 1] = jnp.sum(add_all(terms), axis=1, keepdims=True)

        def blocks(index, carry):
            for half in range(2):
                block(2 * index + half, d_all.at[half])
            return carry

        lax.fori_loop(first // 2, last // 2, blocks, 0)

    def finish_solve(current):
        numer_v[...] = jnp.transpose(sums_v[...])
        curvature = numer_v[2 * DIRS : 3 * DIRS, :] * mask
        weight = 1.0 / (curvature + 1.0)
        return [numer_v[c * DIRS : (c + 1) * DIRS, :] * mask + curvature * current[c] for c in range(2)], weight

    def solve_span(first, last):
        per_load = BLOCKS // LOADS
        while first < last:
            part, offset = divmod(first, per_load)
            if offset == 0:
                loads[part][0].wait()
                loads[part][1].wait()
            end = min(last, (part + 1) * per_load)
            solve_rows(first, end, True)
            first = end

    scatter(lambda peer: send_z.at[peer], recv_z, z_sem, z_peers, z_device, zc)
    recv_z[zc] = send_z[zc]
    start_solve(gains_v[...])
    solve_span(0, FIRST_SPAN)
    wait_bytes(recv_z, N_ZC - 1, z_sem.at[1])
    start_x(0, [recv_z[slot] for slot in range(N_ZC)])
    solve_span(FIRST_SPAN, BLOCKS)
    partial, weight = finish_solve(gains_v)
    for c in range(2):
        work_v[c] = weight * (partial[c] - merged_v[c]) + merged_v[c]
        spare_v[c] = 2.0 * weight - 1.0
    to_owner_rows(work_v, send_w, 0)
    to_owner_rows(spare_v, send_w, 4)
    scatter(lambda peer: send_w.at[peer], recv_w, w_sem, z_peers, z_device, zc)
    recv_w[zc] = send_w[zc]
    start_y(0)

    values = evaluate(0)
    start_g(0, values)
    wait_bytes(recv_w, N_ZC - 1, w_sem.at[1])
    start_x(1, [recv_w[slot, 0:4, :] + recv_w[slot, 4:8, :] * values[slot] for slot in range(N_ZC)])
    start_y(1)
    first = consensus_of(0)
    for c in range(2):
        gain = (partial[c] + 2.0 * first[c] - merged_v[c]) * weight
        spare_v[c] = gain
        merged_v[c] = gain + merged_v[c] - first[c]
    start_solve(spare_v[...])
    solve_rows(0, SECOND_SPAN, False)
    start_g(1, evaluate(1))
    solve_rows(SECOND_SPAN, BLOCKS, False)
    partial, weight = finish_solve(spare_v)
    second = consensus_of(1)
    for c in range(2):
        merged = merged_v[c]
        out_v[0, c] = (partial[c] + 2.0 * second[c] - merged) * weight
        out_v[1, c] = second[c]
        out_v[2, c] = merged - second[c]

    wait_bytes(recv_z, N_ZC - 1, z_sem.at[0])
    wait_bytes(recv_w, N_ZC - 1, w_sem.at[0])
    for turn in range(2):
        wait_bytes(recv_x.at[turn], N_X - 1, x_sem.at[turn, 0])
        wait_bytes(recv_y.at[turn], N_Y - 1, y_sem.at[turn, 0])
        wait_bytes(recv_g.at[turn], N_ZC - 1, g_sem.at[turn, 0])


def write_outputs(results, gains, consensus, duals, sem):
    copies = [
        pltpu.make_async_copy(results.at[place], target.at[0, 0], sem.at[place])
        for place, target in enumerate((gains, consensus, duals))
    ]
    for copy in copies:
        copy.start()
    for copy in copies:
        copy.wait()


def per_device(visibilities, model_vis, station_flags, initial_gains, initial_duals):
    f32 = jnp.float32
    vmem = pl.BlockSpec(memory_space=pltpu.VMEM)
    hbm = pl.BlockSpec(memory_space=pl.ANY)
    results = pl.pallas_call(
        kernel,
        out_shape=jax.ShapeDtypeStruct((3, 2, DIRS, NR), f32),
        in_specs=[hbm] * 5,
        out_specs=vmem,
        scratch_shapes=[
            pltpu.VMEM((DIRS, 2, NR, NR), jnp.bfloat16),
            pltpu.VMEM((2, NR, NR), jnp.bfloat16),
            pltpu.VMEM((DIRS, 2, NR, NR), f32),
            pltpu.VMEM((DIRS, NR, NR), f32),
            pltpu.VMEM((1, NR), jnp.int32),
            pltpu.VMEM((2, DIRS, NR), f32),
            pltpu.VMEM((2, DIRS, NR), f32),
            pltpu.VMEM((2, DIRS, NR), f32),
            pltpu.VMEM((DIRS, NR), f32),
            pltpu.VMEM((NR, LANES), f32),
            pltpu.VMEM((LANES, NR), f32),
            pltpu.VMEM((2, DIRS, 2, ROWS, NR), f32),
            pltpu.VMEM((NR, LANES), f32),
            pltpu.VMEM((LANES, NR), f32),
            pltpu.VMEM((2, DIRS, NR), f32),
            pltpu.VMEM((2, DIRS, NR), f32),
            pltpu.VMEM((2, DIRS, NR), f32),
            pltpu.VMEM((8, LANES), f32),
            pltpu.VMEM((N_ZC, 4, LANES), f32),
            pltpu.VMEM((N_ZC, 4, LANES), f32),
            pltpu.VMEM((N_ZC, 8, LANES), f32),
            pltpu.VMEM((N_ZC, 8, LANES), f32),
            pltpu.VMEM((2, 8, LANES), f32),
            pltpu.VMEM((2, N_X, 8, LANES), f32),
            pltpu.VMEM((2, N_Y, 8, LANES), f32),
            pltpu.VMEM((2, N_Y, 8, LANES), f32),
            pltpu.VMEM((2, N_ZC, 4, LANES), f32),
            pltpu.VMEM((2, N_ZC, 4, LANES), f32),
            pltpu.SemaphoreType.DMA((2, LOADS)),
            pltpu.SemaphoreType.DMA((3,)),
            pltpu.SemaphoreType.DMA((2,)),
            pltpu.SemaphoreType.DMA((2,)),
            pltpu.SemaphoreType.DMA((2, 2)),
            pltpu.SemaphoreType.DMA((2, 2)),
            pltpu.SemaphoreType.DMA((2, 2)),
        ],
        compiler_params=pltpu.CompilerParams(
            collective_id=0, has_side_effects=True, vmem_limit_bytes=60 * 1024 * 1024
        ),
    )(visibilities, model_vis, station_flags, initial_gains, initial_duals)
    block = jax.ShapeDtypeStruct((1, 1, 2, DIRS, NR), f32)
    return pl.pallas_call(
        write_outputs,
        out_shape=(block, block, block),
        in_specs=[vmem],
        out_specs=(hbm, hbm, hbm),
        scratch_shapes=[pltpu.SemaphoreType.DMA((3,))],
        compiler_params=pltpu.CompilerParams(vmem_limit_bytes=1024 * 1024),
    )(results)


def solution(mesh):
    in_specs = (
        P("freq", "tm", None, None, None),
        P("freq", None, None, None, None),
        P("freq", "tm", None),
        P("freq", "tm", None, None, None),
        P("freq", "tm", None, None, None),
    )
    out_specs = (P("freq", "tm", None, None, None),) * 3
    return jax.shard_map(per_device, mesh=mesh, in_specs=in_specs, out_specs=out_specs, check_vma=False)
```

```python
import math

import jax
import jax.numpy as jnp
from jax import lax
from jax.experimental import pallas as pl
from jax.experimental.pallas import tpu as pltpu
from jax.sharding import PartitionSpec as P

DIRS = 8
NR = 512
LANES = 128
TILES = NR // LANES
ROWS = 16
BLOCKS = NR // ROWS
N_Y, N_XH, N_XL, N_ZC = 8, 4, 2, 16
N_X = N_XH * N_XL
N_Z = N_ZC // 2
NF = N_Y * N_XH
NT = N_XL * N_ZC
MESH = pl.DeviceIdType.MESH
SPANS = (0, 8, 20, 32)
SECOND_SPAN = 14
FAR_FIRST = (4, 3, 5, 2, 6, 1, 7)

F0 = 1.0 / math.sqrt(NF)
F1 = 1.0 / math.sqrt(NF * (NF * NF - 1) / 12.0)
F2 = 1.0 / math.sqrt(NF * (NF * NF - 1) * (NF * NF - 4) / 180.0)
F2_SHIFT = (NF * NF - 1) / 12.0
T0 = 1.0 / math.sqrt(NT)
T1 = 1.0 / math.sqrt(NT * (NT * NT - 1) / 12.0)


def tile(index):
    return pl.ds(index * LANES, LANES)


def to_owner_rows(source, target, first_row):
    for lane_tile in range(TILES):
        for pair in range(DIRS // 2):
            for part in range(2):
                target[lane_tile * 4 + pair, first_row + 2 * part : first_row + 2 * part + 2, :] = source[
                    part, 2 * pair : 2 * pair + 2, tile(lane_tile)
                ]


def from_owner_rows(source, target):
    for lane_tile in range(TILES):
        for pair in range(DIRS // 2):
            for part in range(2):
                target[part, 2 * pair : 2 * pair + 2, tile(lane_tile)] = source[
                    lane_tile * 4 + pair, 2 * part : 2 * part + 2, :
                ]


def add_all(terms):
    while len(terms) > 1:
        terms = [a + b for a, b in zip(terms[::2], terms[1::2])] + terms[len(terms) // 2 * 2 :]
    return terms[0]


def kernel(
    vis_hbm, model_hbm, flag_hbm, gains_hbm, duals_hbm,
    out_v,
    model_v, vis_v, wide_v, square_v, flag_v, gains_v, duals_v,
    masked_v, power_v, column_v, stack_v, d_all, sums_v, numer_v, merged_v, work_v, spare_v, eval_v,
    send_z, recv_z, send_w, recv_w, send_x, recv_x, send_y, recv_y, send_g, recv_g,
    load_sem, small_sem, z_sem, w_sem, x_sem, y_sem, g_sem,
):
    freq = lax.axis_index("freq")
    time = lax.axis_index("tm")
    y = freq // N_XH
    x_hi = lax.rem(freq, N_XH)
    x_lo = time // N_ZC
    zc = lax.rem(time, N_ZC)
    x = x_hi * N_XL + x_lo
    z = zc // 2
    core = lax.rem(zc, 2)

    def z_peer(step, flip):
        return lax.rem(z + step, N_Z) * 2 + lax.rem(core + flip, 2)

    z_peers = [z_peer(step, flip) for step in FAR_FIRST for flip in (0, 1)] + [z_peer(0, 1)]
    x_peers = [lax.rem(x + step, N_X) for step in FAR_FIRST]
    y_peers = [lax.rem(y + step, N_Y) for step in FAR_FIRST]

    def z_device(peer):
        return (freq, x_lo * N_ZC + peer)

    def x_device(peer):
        return (y * N_XH + peer // N_XL, lax.rem(peer, N_XL) * N_ZC + zc)

    def y_device(peer):
        return (peer * N_XH + x_hi, time)

    barrier = pltpu.get_barrier_semaphore()
    devices = [z_device(p) for p in z_peers] + [x_device(p) for p in x_peers] + [y_device(p) for p in y_peers]
    small = [
        pltpu.make_async_copy(gains_hbm.at[0, 0], gains_v, small_sem.at[0]),
        pltpu.make_async_copy(duals_hbm.at[0, 0], duals_v, small_sem.at[1]),
        pltpu.make_async_copy(flag_hbm.at[0], flag_v, small_sem.at[2]),
    ]
    for copy in small:
        copy.start()
    for device in devices:
        pl.semaphore_signal(barrier, inc=1, device_id=device, device_id_type=MESH)

    loads = []
    for part, (start, end) in enumerate(zip(SPANS, SPANS[1:])):
        rows = pl.ds(start * ROWS, (end - start) * ROWS)
        model_copy = pltpu.make_async_copy(
            model_hbm.at[0, :, :, rows, :], model_v.at[:, :, rows, :], load_sem.at[0, part]
        )
        vis_copy = pltpu.make_async_copy(vis_hbm.at[0, 0, :, rows, :], vis_v.at[:, rows, :], load_sem.at[1, part])
        model_copy.start()
        vis_copy.start()
        loads.append((model_copy, vis_copy))

    for copy in small:
        copy.wait()
    merged_v[...] = gains_v[...] + duals_v[...]
    to_owner_rows(merged_v, send_z, 0)
    mask = flag_v[...].astype(jnp.float32)

    pl.semaphore_wait(barrier, len(devices))

    def scatter(source, target, sem, peers, device_of, slot):
        for peer in peers:
            pltpu.make_async_remote_copy(
                src_ref=source(peer),
                dst_ref=target.at[slot],
                send_sem=sem.at[0],
                recv_sem=sem.at[1],
                device_id=device_of(peer),
                device_id_type=MESH,
            ).start()

    def wait_bytes(buffer, count, sem):
        part = buffer.at[pl.ds(0, count)]
        pltpu.make_async_copy(part, part, sem).wait()

    def time_moments(parts):
        total = add_all(list(parts))
        ramp = add_all([(slot - (N_ZC - 1) / 2.0) * part for slot, part in enumerate(parts)])
        shift = (x_lo * N_ZC).astype(jnp.float32) - (NT - N_ZC) / 2.0
        return total * T0, (ramp + shift * total) * T1

    def freq_weights(place):
        centre = place.astype(jnp.float32) - (NF - 1) / 2.0
        return F0, centre * F1, (centre * centre - F2_SHIFT) * F2

    def start_x(turn, parts):
        first, second = time_moments(parts)
        send_x[turn, 0:4, :] = first
        send_x[turn, 4:8, :] = second
        scatter(lambda peer: send_x.at[turn], recv_x.at[turn], x_sem.at[turn], x_peers, x_device, x)
        recv_x[turn, x] = send_x[turn]

    def start_y(turn):
        wait_bytes(recv_x.at[turn], N_X - 1, x_sem.at[turn, 1])
        pairs = [recv_x[turn, N_XL * h] + recv_x[turn, N_XL * h + 1] for h in range(N_XH)]
        weights = [freq_weights(y * N_XH + h) for h in range(N_XH)]
        coeffs = [add_all([weights[h][order] * pairs[h] for h in range(N_XH)]) for order in range(3)]
        for peer in range(N_Y):
            there = freq_weights(peer * N_XH + x_hi)
            send_y[turn, peer] = add_all([there[order] * coeffs[order] for order in range(3)])
        scatter(lambda peer: send_y.at[turn, peer], recv_y.at[turn], y_sem.at[turn], y_peers, y_device, y)
        recv_y[turn, y] = send_y[turn, y]

    def evaluate(turn):
        wait_bytes(recv_y.at[turn], N_Y - 1, y_sem.at[turn, 1])
        eval_v[...] = add_all([recv_y[turn, h] for h in range(N_Y)])
        constant = eval_v[0:4, :] * T0
        slope = eval_v[4:8, :] * T1
        shift = (x_lo * N_ZC).astype(jnp.float32) - (NT - 1) / 2.0
        base = constant + shift * slope
        return [base + float(slot) * slope for slot in range(N_ZC)]

    def start_g(turn, values):
        for slot in range(N_ZC):
            send_g[turn, slot] = values[slot]
        scatter(lambda peer: send_g.at[turn, peer], recv_g.at[turn], g_sem.at[turn], z_peers, z_device, zc)
        recv_g[turn, zc] = send_g[turn, zc]

    def consensus_of(turn):
        wait_bytes(recv_g.at[turn], N_ZC - 1, g_sem.at[turn, 1])
        from_owner_rows(recv_g.at[turn], work_v)
        return work_v[...]

    stack_v[...] = jnp.zeros_like(stack_v)
    sums_v[...] = jnp.zeros_like(sums_v)

    def start_solve(current):
        masked_v[...] = current * mask[:, None, :]
        power_v[...] = (current[0] * current[0] + current[1] * current[1]) * mask
        stack_v[0:DIRS, :] = current[0]
        stack_v[DIRS : 2 * DIRS, :] = current[1]
        column_v[...] = jnp.transpose(stack_v[...])

    def solve_rows(first, last, keep):
        def block(index, d_v):
            rows = pl.ds(pl.multiple_of(index * ROWS, ROWS), ROWS)
            column = column_v[rows, :]
            resid = []
            for q in range(TILES):
                pred_real = pred_imag = None
                for k in range(DIRS):
                    if keep:
                        model_real = model_v[k, 0, rows, tile(q)].astype(jnp.float32)
                        model_imag = model_v[k, 1, rows, tile(q)].astype(jnp.float32)
                        wide_v[k, 0, rows, tile(q)] = model_real
                        wide_v[k, 1, rows, tile(q)] = model_imag
                        square_v[k, rows, tile(q)] = model_real * model_real + model_imag * model_imag
                    else:
                        model_real = wide_v[k, 0, rows, tile(q)]
                        model_imag = wide_v[k, 1, rows, tile(q)]
                    row_real = masked_v[0, k : k + 1, tile(q)]
                    row_imag = masked_v[1, k : k + 1, tile(q)]
                    d_real = model_real * row_real + model_imag * row_imag
                    d_imag = model_imag * row_real - model_real * row_imag
                    d_v[k, 0, :, tile(q)] = d_real
                    d_v[k, 1, :, tile(q)] = d_imag
                    col_real = column[:, k : k + 1]
                    col_imag = column[:, DIRS + k : DIRS + k + 1]
                    term_real = col_real * d_real - col_imag * d_imag
                    term_imag = col_real * d_imag + col_imag * d_real
                    pred_real = term_real if pred_real is None else pred_real + term_real
                    pred_imag = term_imag if pred_imag is None else pred_imag + term_imag
                mask_row = mask[:, q * LANES : (q + 1) * LANES]
                resid.append(
                    (
                        vis_v[0, rows, tile(q)].astype(jnp.float32) * mask_row - pred_real,
                        vis_v[1, rows, tile(q)].astype(jnp.float32) * mask_row - pred_imag,
                    )
                )
            for k in range(DIRS):
                numer_real, numer_imag, power = [], [], []
                for q in range(TILES):
                    d_real = d_v[k, 0, :, tile(q)]
                    d_imag = d_v[k, 1, :, tile(q)]
                    resid_real, resid_imag = resid[q]
                    numer_real.append(resid_real * d_real + resid_imag * d_imag)
                    numer_imag.append(resid_imag * d_real - resid_real * d_imag)
                    power.append(square_v[k, rows, tile(q)] * power_v[k : k + 1, tile(q)])
                for place, terms in enumerate((numer_real, numer_imag, power)):
                    lane = place * DIRS + k
                    sums_v[rows, lane : lane + 1] = jnp.sum(add_all(terms), axis=1, keepdims=True)

        def blocks(index, carry):
            for half in range(2):
                block(2 * index + half, d_all.at[half])
            return carry

        lax.fori_loop(first // 2, last // 2, blocks, 0)

    def finish_solve(current):
        numer_v[...] = jnp.transpose(sums_v[...])
        curvature = numer_v[2 * DIRS : 3 * DIRS, :] * mask
        weight = 1.0 / (curvature + 1.0)
        return [numer_v[c * DIRS : (c + 1) * DIRS, :] * mask + curvature * current[c] for c in range(2)], weight

    def solve_span(part):
        loads[part][0].wait()
        loads[part][1].wait()
        solve_rows(SPANS[part], SPANS[part + 1], True)

    scatter(lambda peer: send_z.at[peer], recv_z, z_sem, z_peers, z_device, zc)
    recv_z[zc] = send_z[zc]
    start_solve(gains_v[...])
    solve_span(0)
    solve_span(1)
    wait_bytes(recv_z, N_ZC - 1, z_sem.at[1])
    start_x(0, [recv_z[slot] for slot in range(N_ZC)])
    solve_span(2)
    partial, weight = finish_solve(gains_v)
    for c in range(2):
        work_v[c] = weight * (partial[c] - merged_v[c]) + merged_v[c]
        spare_v[c] = 2.0 * weight - 1.0
    to_owner_rows(work_v, send_w, 0)
    to_owner_rows(spare_v, send_w, 4)
    scatter(lambda peer: send_w.at[peer], recv_w, w_sem, z_peers, z_device, zc)
    recv_w[zc] = send_w[zc]
    start_y(0)

    values = evaluate(0)
    start_g(0, values)
    wait_bytes(recv_w, N_ZC - 1, w_sem.at[1])
    start_x(1, [recv_w[slot, 0:4, :] + recv_w[slot, 4:8, :] * values[slot] for slot in range(N_ZC)])
    start_y(1)
    first = consensus_of(0)
    for c in range(2):
        gain = (partial[c] + 2.0 * first[c] - merged_v[c]) * weight
        spare_v[c] = gain
        merged_v[c] = gain + merged_v[c] - first[c]
    start_solve(spare_v[...])
    solve_rows(0, SECOND_SPAN, False)
    start_g(1, evaluate(1))
    solve_rows(SECOND_SPAN, BLOCKS, False)
    partial, weight = finish_solve(spare_v)
    second = consensus_of(1)
    for c in range(2):
        merged = merged_v[c]
        out_v[0, c] = (partial[c] + 2.0 * second[c] - merged) * weight
        out_v[1, c] = second[c]
        out_v[2, c] = merged - second[c]

    wait_bytes(recv_z, N_ZC - 1, z_sem.at[0])
    wait_bytes(recv_w, N_ZC - 1, w_sem.at[0])
    for turn in range(2):
        wait_bytes(recv_x.at[turn], N_X - 1, x_sem.at[turn, 0])
        wait_bytes(recv_y.at[turn], N_Y - 1, y_sem.at[turn, 0])
        wait_bytes(recv_g.at[turn], N_ZC - 1, g_sem.at[turn, 0])


def write_outputs(results, gains, consensus, duals, sem):
    copies = [
        pltpu.make_async_copy(results.at[place], target.at[0, 0], sem.at[place])
        for place, target in enumerate((gains, consensus, duals))
    ]
    for copy in copies:
        copy.start()
    for copy in copies:
        copy.wait()


def per_device(visibilities, model_vis, station_flags, initial_gains, initial_duals):
    f32 = jnp.float32
    vmem = pl.BlockSpec(memory_space=pltpu.VMEM)
    hbm = pl.BlockSpec(memory_space=pltpu.HBM)
    visibilities, model_vis, station_flags, initial_gains, initial_duals = (
        pltpu.with_memory_space_constraint(array, pltpu.HBM)
        for array in (visibilities, model_vis, station_flags, initial_gains, initial_duals)
    )
    results = pl.pallas_call(
        kernel,
        out_shape=jax.ShapeDtypeStruct((3, 2, DIRS, NR), f32),
        in_specs=[hbm] * 5,
        out_specs=vmem,
        scratch_shapes=[
            pltpu.VMEM((DIRS, 2, NR, NR), jnp.bfloat16),
            pltpu.VMEM((2, NR, NR), jnp.bfloat16),
            pltpu.VMEM((DIRS, 2, NR, NR), f32),
            pltpu.VMEM((DIRS, NR, NR), f32),
            pltpu.VMEM((1, NR), jnp.int32),
            pltpu.VMEM((2, DIRS, NR), f32),
            pltpu.VMEM((2, DIRS, NR), f32),
            pltpu.VMEM((2, DIRS, NR), f32),
            pltpu.VMEM((DIRS, NR), f32),
            pltpu.VMEM((NR, LANES), f32),
            pltpu.VMEM((LANES, NR), f32),
            pltpu.VMEM((2, DIRS, 2, ROWS, NR), f32),
            pltpu.VMEM((NR, LANES), f32),
            pltpu.VMEM((LANES, NR), f32),
            pltpu.VMEM((2, DIRS, NR), f32),
            pltpu.VMEM((2, DIRS, NR), f32),
            pltpu.VMEM((2, DIRS, NR), f32),
            pltpu.VMEM((8, LANES), f32),
            pltpu.VMEM((N_ZC, 4, LANES), f32),
            pltpu.VMEM((N_ZC, 4, LANES), f32),
            pltpu.VMEM((N_ZC, 8, LANES), f32),
            pltpu.VMEM((N_ZC, 8, LANES), f32),
            pltpu.VMEM((2, 8, LANES), f32),
            pltpu.VMEM((2, N_X, 8, LANES), f32),
            pltpu.VMEM((2, N_Y, 8, LANES), f32),
            pltpu.VMEM((2, N_Y, 8, LANES), f32),
            pltpu.VMEM((2, N_ZC, 4, LANES), f32),
            pltpu.VMEM((2, N_ZC, 4, LANES), f32),
            pltpu.SemaphoreType.DMA((2, len(SPANS) - 1)),
            pltpu.SemaphoreType.DMA((3,)),
            pltpu.SemaphoreType.DMA((2,)),
            pltpu.SemaphoreType.DMA((2,)),
            pltpu.SemaphoreType.DMA((2, 2)),
            pltpu.SemaphoreType.DMA((2, 2)),
            pltpu.SemaphoreType.DMA((2, 2)),
        ],
        compiler_params=pltpu.CompilerParams(
            collective_id=0, has_side_effects=True, vmem_limit_bytes=44 * 1024 * 1024
        ),
    )(visibilities, model_vis, station_flags, initial_gains, initial_duals)
    block = jax.ShapeDtypeStruct((1, 1, 2, DIRS, NR), f32)
    return pl.pallas_call(
        write_outputs,
        out_shape=(block, block, block),
        in_specs=[vmem],
        out_specs=(hbm, hbm, hbm),
        scratch_shapes=[pltpu.SemaphoreType.DMA((3,))],
        compiler_params=pltpu.CompilerParams(vmem_limit_bytes=1024 * 1024),
    )(results)


def solution(mesh):
    in_specs = (
        P("freq", "tm", None, None, None),
        P("freq", None, None, None, None),
        P("freq", "tm", None),
        P("freq", "tm", None, None, None),
        P("freq", "tm", None, None, None),
    )
    out_specs = (P("freq", "tm", None, None, None),) * 3
    return jax.shard_map(per_device, mesh=mesh, in_specs=in_specs, out_specs=out_specs, check_vma=False)
```
